256 devices in a mesh: row: 16 (over z, core), col: 16 (over x, y).
Axes of the slice: x: 4, y: 4, z: 8, core: 2. Of those that a mesh axis runs over, the one named last changes fastest.
Arguments:
- factor: float32 [1, 16, 896, 1, 16, 896], P(None, 'row', None, None, 'col'), as said below
- damping: float32 [1], replicated, may hold values from 0.1 to 1
Outputs:
- factor_state: float32 [1, 16, 896, 1, 16, 896], P(None, 'row', None, None, 'col')
The draws below stay inside these ranges and needn't reach their ends.
Inputs may be any that keep to these rules, and one draw needn't show every extreme that they name: factor is symmetric and positive semidefinite, so that A's smallest eigenvalue is at least damping[0].
All inputs are finite; a program needn't handle non-finite values.
Results may differ from the reference program's by a relative error of at most 0.00016.
Values sent between devices are 32-bit elements; how exact they have to be, the bound alone decides.
No kernel may reach another device: no remote copies, remote signals or barrier semaphores. Data moves between devices by JAX's collectives and lax.ppermute only.
A program may use at most 128 MiB of HBM per device.

```python
import math
import jax
import jax.numpy as jnp
from jax import lax

B = 896
NT = 16
PANELS = 1
GR = 16
GC = 16
TR = 1
TC = 1


def draw_factor(key, part):
    full_order = B * NT
    samples = 4 * B
    key_noise, key_weight = jax.random.split(jax.random.fold_in(key, 11), 2)
    noise_part = jax.random.truncated_normal(key_noise, -3.0, 3.0, (full_order, samples), jnp.float32)
    log_weight = jax.random.uniform(key_weight, (samples,), jnp.float32, math.log(0.1), math.log(10.0))
    columns = noise_part
    weights = jnp.exp(log_weight)
    scaled = columns * jnp.sqrt(weights / jnp.sum(weights))[None, :]
    product = jnp.dot(scaled, scaled.T, precision=lax.Precision.HIGHEST, preferred_element_type=jnp.float32)
    symmetric = 0.5 * (product + product.T)
    return symmetric.reshape(TR, GR, B, TC, GC, B)


def draw_damping(key, part):
    return jax.random.uniform(jax.random.fold_in(key, 23), (1,), jnp.float32, 0.1, 1.0)


def setup_inputs(seed: int = 0) -> dict:
    arg_keys = jax.random.split(jax.random.key(seed), 3)
    return {
        "factor": draw_factor(jax.random.fold_in(arg_keys[2], 71), 0),
        "damping": draw_damping(jax.random.fold_in(arg_keys[2], 71), 0),
    }


def times_transposed(left, right):
    return lax.dot_general(left, right, (((1,), (1,)), ((), ())), precision=lax.Precision.HIGHEST)

def reference(factor, damping):
    full_order = B * NT
    matrix = factor.reshape(full_order, full_order)
    positions = jnp.arange(full_order, dtype=jnp.int32)
    on_diagonal = (positions[:, None] == positions[None, :]).astype(matrix.dtype)
    current = matrix + damping[0] * on_diagonal
    tile_identity = jnp.eye(B, dtype=matrix.dtype)
    for step_index in range(PANELS):
        start_row = step_index * B
        end_row = start_row + B
        diag_lower = jnp.linalg.cholesky(current[start_row:end_row, start_row:end_row])
        inverse = jax.scipy.linalg.solve_triangular(diag_lower, tile_identity, lower=True)
        panel_block = times_transposed(current[end_row:, start_row:end_row], inverse)
        trailing = current[end_row:, end_row:] - times_transposed(panel_block, panel_block)
        current = current.at[end_row:, end_row:].set(trailing)
        column = jnp.concatenate([jnp.zeros((start_row, B), matrix.dtype), diag_lower, panel_block], axis=0)
        current = current.at[:, start_row:end_row].set(column)
    tile_of = positions // B
    result = jnp.where(tile_of[:, None] >= tile_of[None, :], current, jnp.zeros_like(current))
    return result.reshape(TR, GR, B, TC, GC, B)
```

```python
import jax
import jax.numpy as jnp
from jax import lax
from jax.experimental import pallas as pl
from jax.experimental.pallas import tpu as pltpu
from jax.sharding import PartitionSpec as P

F32 = jnp.float32
BF16 = jnp.bfloat16
ORDER = 896
LANES = 128
BLOCKS = ORDER // LANES
FLAT = ORDER * BLOCKS
GRID = 16
PIECE = FLAT // GRID
GROUPS = ((0, 256), (256, 512), (512, 768), (768, 896))
INTERPRET = False


def split(value):
    high = value.astype(BF16)
    return high, (value - high.astype(F32)).astype(BF16)


def product(left, right, transposed):
    dims = (((1,), (1 if transposed else 0,)), ((), ()))
    return lax.dot_general(left, right, dims, preferred_element_type=F32)


def product3(left, right, transposed=False):
    (left_high, left_low), (right_high, right_low) = left, right
    return product(left_high, right_high, transposed) + (
        product(left_high, right_low, transposed) + product(left_low, right_high, transposed)
    )


def factor_block(rows):
    lane = lax.broadcasted_iota(jnp.int32, (8, LANES), 1)
    sublane = lax.broadcasted_iota(jnp.int32, (8, LANES), 0)

    def lane_of(value, index):
        return jnp.broadcast_to(value[:, index:index + 1], (8, LANES))

    def row_of(value, index):
        return jnp.broadcast_to(value[index:index + 1, :], (8, LANES))

    rows = list(rows)
    mixed, corner = [], []
    for slab in range(16):
        base = 8 * slab
        own = (lane >= base) & (lane < base + 8)
        pivot_rows = rows[slab]
        columns = [lane_of(pivot_rows, base + m) for m in range(8)]
        diag_rows = jnp.where(own, pivot_rows, 0.0)
        pivot_rows = jnp.where(own, jnp.where(lane - base == sublane, 1.0, 0.0), pivot_rows)
        mixed_slab = jnp.zeros((8, LANES), F32)
        corner_slab = jnp.zeros((8, LANES), F32)
        for j in range(8):
            pivot = row_of(columns[j], j)
            root = lax.rsqrt(pivot)
            inverse = 1.0 / pivot
            is_j = sublane == j
            factor = jnp.where(is_j, 1.0 - inverse, columns[j] * inverse)
            mixed_slab = jnp.where(is_j, pivot_rows * root, mixed_slab)
            corner_slab = jnp.where(is_j, diag_rows * root, corner_slab)
            for m in range(j + 1, 8):
                columns[m] = columns[m] - factor * row_of(columns[m], j)
            pivot_rows = pivot_rows - factor * row_of(pivot_rows, j)
            if j < 7:
                diag_rows = diag_rows - factor * row_of(diag_rows, j)
        mixed.append(mixed_slab)
        corner.append(corner_slab)
        spread = [row_of(pivot_rows, m) for m in range(8)]
        for other in range(slab + 1, 16):
            old = rows[other]
            new = jnp.where(own, 0.0, old)
            for m in range(8):
                new = new - lane_of(old, base + m) * spread[m]
            rows[other] = new
    return mixed, corner


def factor_kernel(damping_ref, tile_ref, high_ref, low_ref, upper_ref, work):
    damping = damping_ref[0]
    row_id = lax.broadcasted_iota(jnp.int32, (ORDER, LANES), 0)
    lane_id = lax.broadcasted_iota(jnp.int32, (ORDER, LANES), 1)
    for block in range(BLOCKS):
        values = tile_ref[pl.ds(block, ORDER, stride=BLOCKS), :]
        on_diagonal = row_id == lane_id + LANES * block
        work[:, LANES * block:LANES * (block + 1)] = jnp.where(on_diagonal, values + damping, values)
    lane = lax.broadcasted_iota(jnp.int32, (8, LANES), 1)

    def step(k, carry):
        start = pl.multiple_of(k * LANES, LANES)
        here = pl.ds(start, LANES)
        slabs = [work[pl.ds(start + 8 * i, 8), here] for i in range(16)]
        mixed, corner = factor_block(slabs)
        inverse = jnp.concatenate([jnp.where(lane < 8 * i + 8, mixed[i], 0.0) for i in range(16)], axis=0)
        upper = jnp.concatenate([jnp.where(lane < 8 * i + 8, corner[i], mixed[i]) for i in range(16)], axis=0)
        inverse_parts = split(inverse)
        work[here, :] = product3(inverse_parts, split(work[here, :]))
        upper_ref[here, :] = work[here, :]
        upper_ref[here, here] = upper
        work[here, here] = inverse
        panel_parts = split(work[here, :])

        def update(i, inner):
            there = pl.ds(pl.multiple_of(i * LANES, LANES), LANES)
            column = product3(split(work[there, here]), inverse_parts, transposed=True)
            work[there, here] = jnp.zeros((LANES, LANES), F32)
            work[there, :] = work[there, :] - product3(split(column), panel_parts)
            return inner

        lax.fori_loop(k + 1, BLOCKS, update, 0)
        return carry

    lax.fori_loop(0, BLOCKS, step, 0)
    for i in range(BLOCKS):
        down = slice(LANES * i, LANES * (i + 1))
        row_id = lax.broadcasted_iota(jnp.int32, (LANES, ORDER), 0) + LANES * i
        col_id = lax.broadcasted_iota(jnp.int32, (LANES, ORDER), 1)
        high, low = split(jnp.where(col_id <= row_id, work[down, :], 0.0))
        high_ref[down, :] = high
        low_ref[down, :] = low


def update_kernel(
    where_ref, damping_ref, high_ref, low_ref, upper_ref, row_ref, col_ref, own_ref, out_ref,
    row_high, row_low, col_high, col_low, left_high, left_low,
):
    row, col = where_ref[0], where_ref[1]

    def load(ref, high, low):
        for block in range(BLOCKS):
            lanes = slice(LANES * block, LANES * (block + 1))
            high[:, lanes], low[:, lanes] = split(ref[pl.ds(block, ORDER, stride=BLOCKS), :])

    @pl.when(row < col)
    def _():
        out_ref[...] = jnp.zeros((FLAT, LANES), F32)

    @pl.when(jnp.logical_and(row == 0, col == 0))
    def _():
        row_id = lax.broadcasted_iota(jnp.int32, (ORDER, LANES), 0)
        lane_id = lax.broadcasted_iota(jnp.int32, (ORDER, LANES), 1)
        for block in range(BLOCKS):
            lower = upper_ref[LANES * block:LANES * (block + 1), :].T
            keep = row_id >= lane_id + LANES * block
            out_ref[pl.ds(block, ORDER, stride=BLOCKS), :] = jnp.where(keep, lower, 0.0)

    @pl.when(jnp.logical_and(row > 0, col == 0))
    def _():
        load(own_ref, row_high, row_low)
        for start, stop in GROUPS:
            left = row_high[:, :stop], row_low[:, :stop]
            result = product3(left, (high_ref[start:stop, :stop], low_ref[start:stop, :stop]), transposed=True)
            for block in range(start // LANES, stop // LANES):
                at = LANES * block - start
                out_ref[pl.ds(block, ORDER, stride=BLOCKS), :] = result[:, at:at + LANES]

    @pl.when(jnp.logical_and(row >= col, col > 0))
    def _():
        load(row_ref, row_high, row_low)
        load(col_ref, col_high, col_low)
        for start, stop in reversed(GROUPS):
            weights = high_ref[start:stop, :stop], low_ref[start:stop, :stop]
            solved = product3(weights, (row_high[:stop, :], row_low[:stop, :]))
            left_high[:, start:stop], left_low[:, start:stop] = split(solved.T)
            solved = product3(weights, (col_high[:stop, :], col_low[:stop, :]))
            col_high[start:stop, :], col_low[start:stop, :] = split(solved)
        added = jnp.where(row == col, damping_ref[0], 0.0)
        row_id = lax.broadcasted_iota(jnp.int32, (ORDER, LANES), 0)
        lane_id = lax.broadcasted_iota(jnp.int32, (ORDER, LANES), 1)
        for start, stop in GROUPS:
            left = left_high[...], left_low[...]
            result = product3(left, (col_high[:, start:stop], col_low[:, start:stop]))
            for block in range(start // LANES, stop // LANES):
                at = LANES * block - start
                place = pl.ds(block, ORDER, stride=BLOCKS)
                own = own_ref[place, :]
                own = jnp.where(row_id == lane_id + LANES * block, own + added, own)
                out_ref[place, :] = own - result[:, at:at + LANES]


VMEM = pl.BlockSpec(memory_space=pltpu.VMEM)
SMEM = pl.BlockSpec(memory_space=pltpu.SMEM)


def factorize(damping, tile):
    return pl.pallas_call(
        factor_kernel,
        out_shape=[
            jax.ShapeDtypeStruct((ORDER, ORDER), BF16),
            jax.ShapeDtypeStruct((ORDER, ORDER), BF16),
            jax.ShapeDtypeStruct((ORDER, ORDER), F32),
        ],
        in_specs=[SMEM, VMEM],
        out_specs=[VMEM, VMEM, VMEM],
        scratch_shapes=[pltpu.VMEM((ORDER, ORDER), F32)],
        interpret=INTERPRET,
        name="factorize",
    )(damping, tile)


def finish(where, damping, high, low, upper, row_tile, col_tile, own):
    return pl.pallas_call(
        update_kernel,
        out_shape=jax.ShapeDtypeStruct((FLAT, LANES), F32),
        in_specs=[SMEM, SMEM] + [VMEM] * 6,
        out_specs=VMEM,
        scratch_shapes=[pltpu.VMEM((ORDER, ORDER), BF16)] * 6,
        interpret=INTERPRET,
        name="finish",
    )(where, damping, high, low, upper, row_tile, col_tile, own)


def on_device(factor, damping):
    row = lax.axis_index("row")
    col = lax.axis_index("col")
    own = factor.reshape(FLAT, LANES)

    piece = jnp.where(row == 0, own[:PIECE], 0.0)
    arrived = [
        lax.ppermute(own[PIECE * r:PIECE * (r + 1)], "row", [(0, r)]) for r in range(1, GRID)
    ]
    for other in arrived:
        piece = piece + other

    first = jnp.where(col == 0, piece, 0.0)
    for hop in (8, 4, 2, 1):
        pairs = [(c, c + hop) for c in range(0, GRID, 2 * hop)]
        first = first + lax.ppermute(first, "col", pairs)

    swap = [(r * GRID + c, c * GRID + r) for r in range(GRID) for c in range(GRID)]
    turned = lax.ppermute(piece, ("row", "col"), swap)

    col_tile = lax.all_gather(piece, "row", axis=0, tiled=True)
    first_tile = lax.all_gather(first, "row", axis=0, tiled=True)
    row_tile = lax.all_gather(turned, "col", axis=0, tiled=True)

    high, low, upper = factorize(damping, first_tile)
    where = jnp.stack([row, col]).astype(jnp.int32)
    result = finish(where, damping, high, low, upper, row_tile, col_tile, own)
    return result.reshape(factor.shape)


def solution(mesh):
    return jax.shard_map(
        on_device,
        mesh=mesh,
        in_specs=(P(None, "row", None, None, "col", None), P()),
        out_specs=P(None, "row", None, None, "col", None),
        check_vma=False,
    )
```

```python
import jax
import jax.numpy as jnp
from jax import lax
from jax.experimental import pallas as pl
from jax.experimental.pallas import tpu as pltpu
from jax.sharding import PartitionSpec as P

F32 = jnp.float32
BF16 = jnp.bfloat16
ORDER = 896
LANES = 128
BLOCKS = ORDER // LANES
FLAT = ORDER * BLOCKS
GRID = 16
CHIPS = GRID // 2
PAIR_ROWS = ORDER // CHIPS
GROUPS = ((0, 256), (256, 512), (512, 768), (768, 896))
INTERPRET = False


def split(value):
    high = value.astype(BF16)
    return high, (value - high.astype(F32)).astype(BF16)


def product(left, right, transposed):
    dims = (((1,), (1 if transposed else 0,)), ((), ()))
    return lax.dot_general(left, right, dims, preferred_element_type=F32)


def product3(left, right, transposed=False):
    (left_high, left_low), (right_high, right_low) = left, right
    return product(left_high, right_high, transposed) + (
        product(left_high, right_low, transposed) + product(left_low, right_high, transposed)
    )


def factor_block(rows):
    lane = lax.broadcasted_iota(jnp.int32, (8, LANES), 1)
    sublane = lax.broadcasted_iota(jnp.int32, (8, LANES), 0)

    def lane_of(value, index):
        return jnp.broadcast_to(value[:, index:index + 1], (8, LANES))

    def row_of(value, index):
        return jnp.broadcast_to(value[index:index + 1, :], (8, LANES))

    rows = list(rows)
    mixed, corner = [], []
    for slab in range(16):
        base = 8 * slab
        own = (lane >= base) & (lane < base + 8)
        pivot_rows = rows[slab]
        columns = [lane_of(pivot_rows, base + m) for m in range(8)]
        diag_rows = jnp.where(own, pivot_rows, 0.0)
        pivot_rows = jnp.where(own, jnp.where(lane - base == sublane, 1.0, 0.0), pivot_rows)
        mixed_slab = jnp.zeros((8, LANES), F32)
        corner_slab = jnp.zeros((8, LANES), F32)
        for j in range(8):
            pivot = row_of(columns[j], j)
            root = lax.rsqrt(pivot)
            inverse = 1.0 / pivot
            is_j = sublane == j
            factor = jnp.where(is_j, 1.0 - inverse, columns[j] * inverse)
            mixed_slab = jnp.where(is_j, pivot_rows * root, mixed_slab)
            corner_slab = jnp.where(is_j, diag_rows * root, corner_slab)
            for m in range(j + 1, 8):
                columns[m] = columns[m] - factor * row_of(columns[m], j)
            pivot_rows = pivot_rows - factor * row_of(pivot_rows, j)
            if j < 7:
                diag_rows = diag_rows - factor * row_of(diag_rows, j)
        mixed.append(mixed_slab)
        corner.append(corner_slab)
        spread = [row_of(pivot_rows, m) for m in range(8)]
        for other in range(slab + 1, 16):
            old = rows[other]
            new = jnp.where(own, 0.0, old)
            for m in range(8):
                new = new - lane_of(old, base + m) * spread[m]
            rows[other] = new
    return mixed, corner


def factor_kernel(where_ref, damping_ref, *refs):
    pair_refs, (high_ref, low_ref, upper_ref, work) = refs[:CHIPS], refs[CHIPS:]
    damping = damping_ref[0]
    chip = where_ref[0] // 2
    sign = 1 - 2 * (where_ref[0] % 2)
    row_id = lax.broadcasted_iota(jnp.int32, (PAIR_ROWS, LANES), 0)
    lane_id = lax.broadcasted_iota(jnp.int32, (PAIR_ROWS, LANES), 1)
    for index, ref in enumerate(pair_refs):
        hop = (index + 1) // 2
        source = (chip + (-sign if index % 2 else sign) * hop + CHIPS) % CHIPS
        start = pl.multiple_of(source * PAIR_ROWS, PAIR_ROWS)
        for block in range(BLOCKS):
            values = ref[pl.ds(block, PAIR_ROWS, stride=BLOCKS), :]
            on_diagonal = row_id + start == lane_id + LANES * block
            work[pl.ds(start, PAIR_ROWS), LANES * block:LANES * (block + 1)] = jnp.where(
                on_diagonal, values + damping, values
            )
    lane = lax.broadcasted_iota(jnp.int32, (8, LANES), 1)

    def step(k, carry):
        start = pl.multiple_of(k * LANES, LANES)
        here = pl.ds(start, LANES)
        slabs = [work[pl.ds(start + 8 * i, 8), here] for i in range(16)]
        mixed, corner = factor_block(slabs)
        inverse = jnp.concatenate([jnp.where(lane < 8 * i + 8, mixed[i], 0.0) for i in range(16)], axis=0)
        upper = jnp.concatenate([jnp.where(lane < 8 * i + 8, corner[i], mixed[i]) for i in range(16)], axis=0)
        inverse_parts = split(inverse)
        work[here, :] = product3(inverse_parts, split(work[here, :]))
        upper_ref[here, :] = work[here, :]
        upper_ref[here, here] = upper
        work[here, here] = inverse
        panel_parts = split(work[here, :])

        def update(i, inner):
            there = pl.ds(pl.multiple_of(i * LANES, LANES), LANES)
            column = product3(split(work[there, here]), inverse_parts, transposed=True)
            work[there, here] = jnp.zeros((LANES, LANES), F32)
            work[there, :] = work[there, :] - product3(split(column), panel_parts)
            return inner

        lax.fori_loop(k + 1, BLOCKS, update, 0)
        return carry

    lax.fori_loop(0, BLOCKS, step, 0)
    for i in range(BLOCKS):
        down = slice(LANES * i, LANES * (i + 1))
        row_id = lax.broadcasted_iota(jnp.int32, (LANES, ORDER), 0) + LANES * i
        col_id = lax.broadcasted_iota(jnp.int32, (LANES, ORDER), 1)
        high, low = split(jnp.where(col_id <= row_id, work[down, :], 0.0))
        high_ref[down, :] = high
        low_ref[down, :] = low


def update_kernel(
    where_ref, damping_ref, high_ref, low_ref, upper_ref, row_ref, col_ref, own_ref, out_ref,
    row_high, row_low, col_high, col_low, left_high, left_low,
):
    row, col = where_ref[0], where_ref[1]

    def load(ref, high, low):
        for block in range(BLOCKS):
            lanes = slice(LANES * block, LANES * (block + 1))
            high[:, lanes], low[:, lanes] = split(ref[pl.ds(block, ORDER, stride=BLOCKS), :])

    @pl.when(row < col)
    def _():
        out_ref[...] = jnp.zeros((FLAT, LANES), F32)

    @pl.when(jnp.logical_and(row == 0, col == 0))
    def _():
        row_id = lax.broadcasted_iota(jnp.int32, (ORDER, LANES), 0)
        lane_id = lax.broadcasted_iota(jnp.int32, (ORDER, LANES), 1)
        for block in range(BLOCKS):
            lower = upper_ref[LANES * block:LANES * (block + 1), :].T
            keep = row_id >= lane_id + LANES * block
            out_ref[pl.ds(block, ORDER, stride=BLOCKS), :] = jnp.where(keep, lower, 0.0)

    @pl.when(jnp.logical_and(row > 0, col == 0))
    def _():
        load(own_ref, row_high, row_low)
        for start, stop in GROUPS:
            left = row_high[:, :stop], row_low[:, :stop]
            result = product3(left, (high_ref[start:stop, :stop], low_ref[start:stop, :stop]), transposed=True)
            for block in range(start // LANES, stop // LANES):
                at = LANES * block - start
                out_ref[pl.ds(block, ORDER, stride=BLOCKS), :] = result[:, at:at + LANES]

    @pl.when(jnp.logical_and(row >= col, col > 0))
    def _():
        load(row_ref, row_high, row_low)
        load(col_ref, col_high, col_low)
        for start, stop in reversed(GROUPS):
            weights = high_ref[start:stop, :stop], low_ref[start:stop, :stop]
            solved = product3(weights, (row_high[:stop, :], row_low[:stop, :]))
            left_high[:, start:stop], left_low[:, start:stop] = split(solved.T)
            solved = product3(weights, (col_high[:stop, :], col_low[:stop, :]))
            col_high[start:stop, :], col_low[start:stop, :] = split(solved)
        added = jnp.where(row == col, damping_ref[0], 0.0)
        row_id = lax.broadcasted_iota(jnp.int32, (ORDER, LANES), 0)
        lane_id = lax.broadcasted_iota(jnp.int32, (ORDER, LANES), 1)
        for start, stop in GROUPS:
            left = left_high[...], left_low[...]
            result = product3(left, (col_high[:, start:stop], col_low[:, start:stop]))
            for block in range(start // LANES, stop // LANES):
                at = LANES * block - start
                place = pl.ds(block, ORDER, stride=BLOCKS)
                own = own_ref[place, :]
                own = jnp.where(row_id == lane_id + LANES * block, own + added, own)
                out_ref[place, :] = own - result[:, at:at + LANES]


VMEM = pl.BlockSpec(memory_space=pltpu.VMEM)
SMEM = pl.BlockSpec(memory_space=pltpu.SMEM)


def factorize(where, damping, pairs):
    return pl.pallas_call(
        factor_kernel,
        out_shape=[
            jax.ShapeDtypeStruct((ORDER, ORDER), BF16),
            jax.ShapeDtypeStruct((ORDER, ORDER), BF16),
            jax.ShapeDtypeStruct((ORDER, ORDER), F32),
        ],
        in_specs=[SMEM, SMEM] + [VMEM] * CHIPS,
        out_specs=[VMEM, VMEM, VMEM],
        scratch_shapes=[pltpu.VMEM((ORDER, ORDER), F32)],
        interpret=INTERPRET,
        name="factorize",
    )(where, damping, *pairs)


def finish(where, damping, high, low, upper, row_tile, col_tile, own):
    return pl.pallas_call(
        update_kernel,
        out_shape=jax.ShapeDtypeStruct((FLAT, LANES), F32),
        in_specs=[SMEM, SMEM] + [VMEM] * 6,
        out_specs=VMEM,
        scratch_shapes=[pltpu.VMEM((ORDER, ORDER), BF16)] * 6,
        interpret=INTERPRET,
        name="finish",
    )(where, damping, high, low, upper, row_tile, col_tile, own)


def spread(own):
    row = lax.axis_index("row")
    col = lax.axis_index("col")
    core = row % 2
    size = own.shape[0] // GRID

    piece = jnp.where(row == 0, own[:size], 0.0)
    arrived = [
        lax.ppermute(own[size * r:size * (r + 1)], "row", [(0, r)]) for r in range(1, GRID)
    ]
    for other in arrived:
        piece = piece + other

    swap = [(r * GRID + c, c * GRID + r) for r in range(GRID) for c in range(GRID)]
    turned = lax.ppermute(piece, ("row", "col"), swap)
    row_tile = lax.all_gather(turned, "col", axis=0, tiled=True)
    col_tile = lax.all_gather(piece, "row", axis=0, tiled=True)

    first = jnp.where(col == 0, piece, 0.0)
    for hop in (8, 4, 2, 1):
        pairs = [(c, c + hop) for c in range(0, GRID, 2 * hop)]
        first = first + lax.ppermute(first, "col", pairs)

    chips = GRID // 2
    other_core = [(r, r ^ 1) for r in range(GRID)]
    onward = [(2 * z, 2 * ((z + 1) % chips)) for z in range(chips)]
    onward += [(2 * z + 1, 2 * ((z - 1) % chips) + 1) for z in range(chips)]
    partner = lax.ppermute(first, "row", other_core)
    moving = jnp.concatenate(
        [jnp.where(core == 0, first, partner), jnp.where(core == 0, partner, first)], axis=0
    )
    pairs = [moving]
    for hop in range(1, chips // 2 + 1):
        moving = lax.ppermute(moving, "row", onward)
        pairs.append(moving)
        if hop < chips // 2:
            pairs.append(lax.ppermute(moving, "row", other_core))
    return pairs, row_tile, col_tile


def on_device(factor, damping):
    row = lax.axis_index("row")
    col = lax.axis_index("col")
    own = factor.reshape(FLAT, LANES)
    pairs, row_tile, col_tile = spread(own)
    where = jnp.stack([row, col]).astype(jnp.int32)
    high, low, upper = factorize(where, damping, pairs)
    result = finish(where, damping, high, low, upper, row_tile, col_tile, own)
    return result.reshape(factor.shape)


def solution(mesh):
    return jax.shard_map(
        on_device,
        mesh=mesh,
        in_specs=(P(None, "row", None, None, "col", None), P()),
        out_specs=P(None, "row", None, None, "col", None),
        check_vma=False,
    )
```

```python
import jax
import jax.numpy as jnp
from jax import lax
from jax.experimental import pallas as pl
from jax.experimental.pallas import tpu as pltpu
from jax.sharding import PartitionSpec as P


F32 = jnp.float32
BF16 = jnp.bfloat16
ORDER = 896
LANES = 128
BLOCKS = ORDER // LANES
FLAT = ORDER * BLOCKS
GRID = 16
CHIPS = GRID // 2
PAIR_ROWS = ORDER // CHIPS
GROUPS = ((0, 256), (256, 512), (512, 768), (768, 896))
SCATTER = (4, 3, 5, 2, 6, 1, 7)
INTERPRET = False


def split(value):
    high = value.astype(BF16)
    return high, (value - high.astype(F32)).astype(BF16)


def product(left, right, transposed):
    dims = (((1,), (1 if transposed else 0,)), ((), ()))
    return lax.dot_general(left, right, dims, preferred_element_type=F32)


def product3(left, right, transposed=False):
    (left_high, left_low), (right_high, right_low) = left, right
    return product(left_high, right_high, transposed) + (
        product(left_high, right_low, transposed) + product(left_low, right_high, transposed)
    )


def factor_block(rows):
    lane = lax.broadcasted_iota(jnp.int32, (8, LANES), 1)
    sublane = lax.broadcasted_iota(jnp.int32, (8, LANES), 0)

    def lane_of(value, index):
        return jnp.broadcast_to(value[:, index:index + 1], (8, LANES))

    def row_of(value, index):
        return jnp.broadcast_to(value[index:index + 1, :], (8, LANES))

    rows = list(rows)
    mixed, corner = [], []
    for slab in range(16):
        base = 8 * slab
        own = (lane >= base) & (lane < base + 8)
        pivot_rows = rows[slab]
        columns = [lane_of(pivot_rows, base + m) for m in range(8)]
        diag_rows = jnp.where(own, pivot_rows, 0.0)
        pivot_rows = jnp.where(own, jnp.where(lane - base == sublane, 1.0, 0.0), pivot_rows)
        mixed_slab = jnp.zeros((8, LANES), F32)
        corner_slab = jnp.zeros((8, LANES), F32)
        for j in range(8):
            pivot = row_of(columns[j], j)
            root = lax.rsqrt(pivot)
            inverse = 1.0 / pivot
            is_j = sublane == j
            factor = jnp.where(is_j, 1.0 - inverse, columns[j] * inverse)
            mixed_slab = jnp.where(is_j, pivot_rows * root, mixed_slab)
            corner_slab = jnp.where(is_j, diag_rows * root, corner_slab)
            for m in range(j + 1, 8):
                columns[m] = columns[m] - factor * row_of(columns[m], j)
            pivot_rows = pivot_rows - factor * row_of(pivot_rows, j)
            if j < 7:
                diag_rows = diag_rows - factor * row_of(diag_rows, j)
        mixed.append(mixed_slab)
        corner.append(corner_slab)
        spread = [row_of(pivot_rows, m) for m in range(8)]
        for other in range(slab + 1, 16):
            old = rows[other]
            new = jnp.where(own, 0.0, old)
            for m in range(8):
                new = new - lane_of(old, base + m) * spread[m]
            rows[other] = new
    return mixed, corner


def factor_kernel(where_ref, damping_ref, *refs):
    pair_refs, (high_ref, low_ref, upper_ref, work) = refs[:CHIPS], refs[CHIPS:]
    damping = damping_ref[0]
    chip = where_ref[0] // 2
    sign = 1 - 2 * (where_ref[0] % 2)
    row_id = lax.broadcasted_iota(jnp.int32, (PAIR_ROWS, LANES), 0)
    lane_id = lax.broadcasted_iota(jnp.int32, (PAIR_ROWS, LANES), 1)
    for index, ref in enumerate(pair_refs):
        hop = (index + 1) // 2
        source = (chip + (-sign if index % 2 else sign) * hop + CHIPS) % CHIPS
        start = pl.multiple_of(source * PAIR_ROWS, PAIR_ROWS)
        for block in range(BLOCKS):
            values = ref[pl.ds(block, PAIR_ROWS, stride=BLOCKS), :]
            on_diagonal = row_id + start == lane_id + LANES * block
            work[pl.ds(start, PAIR_ROWS), LANES * block:LANES * (block + 1)] = jnp.where(
                on_diagonal, values + damping, values
            )
    lane = lax.broadcasted_iota(jnp.int32, (8, LANES), 1)

    def step(k, carry):
        start = pl.multiple_of(k * LANES, LANES)
        here = pl.ds(start, LANES)
        slabs = [work[pl.ds(start + 8 * i, 8), here] for i in range(16)]
        mixed, corner = factor_block(slabs)
        inverse = jnp.concatenate([jnp.where(lane < 8 * i + 8, mixed[i], 0.0) for i in range(16)], axis=0)
        upper = jnp.concatenate([jnp.where(lane < 8 * i + 8, corner[i], mixed[i]) for i in range(16)], axis=0)
        inverse_parts = split(inverse)
        work[here, :] = product3(inverse_parts, split(work[here, :]))
        upper_ref[here, :] = work[here, :]
        upper_ref[here, here] = upper
        work[here, here] = inverse
        panel_parts = split(work[here, :])

        def update(i, inner):
            there = pl.ds(pl.multiple_of(i * LANES, LANES), LANES)
            column = product3(split(work[there, here]), inverse_parts, transposed=True)
            work[there, here] = jnp.zeros((LANES, LANES), F32)
            work[there, :] = work[there, :] - product3(split(column), panel_parts)
            return inner

        lax.fori_loop(k + 1, BLOCKS, update, 0)
        return carry

    lax.fori_loop(0, BLOCKS, step, 0)
    for i in range(BLOCKS):
        down = slice(LANES * i, LANES * (i + 1))
        row_id = lax.broadcasted_iota(jnp.int32, (LANES, ORDER), 0) + LANES * i
        col_id = lax.broadcasted_iota(jnp.int32, (LANES, ORDER), 1)
        high, low = split(jnp.where(col_id <= row_id, work[down, :], 0.0))
        high_ref[down, :] = high
        low_ref[down, :] = low


def update_kernel(
    where_ref, damping_ref, high_ref, low_ref, upper_ref, row_ref, col_ref, own_ref, out_ref,
    row_high, row_low, col_high, col_low, left_high, left_low,
):
    row, col = where_ref[0], where_ref[1]

    def load(ref, high, low):
        for block in range(BLOCKS):
            lanes = slice(LANES * block, LANES * (block + 1))
            high[:, lanes], low[:, lanes] = split(ref[pl.ds(block, ORDER, stride=BLOCKS), :])

    @pl.when(row < col)
    def _():
        out_ref[...] = jnp.zeros((FLAT, LANES), F32)

    @pl.when(jnp.logical_and(row == 0, col == 0))
    def _():
        row_id = lax.broadcasted_iota(jnp.int32, (ORDER, LANES), 0)
        lane_id = lax.broadcasted_iota(jnp.int32, (ORDER, LANES), 1)
        for block in range(BLOCKS):
            lower = upper_ref[LANES * block:LANES * (block + 1), :].T
            keep = row_id >= lane_id + LANES * block
            out_ref[pl.ds(block, ORDER, stride=BLOCKS), :] = jnp.where(keep, lower, 0.0)

    @pl.when(jnp.logical_and(row > 0, col == 0))
    def _():
        load(own_ref, row_high, row_low)
        for start, stop in GROUPS:
            left = row_high[:, :stop], row_low[:, :stop]
            result = product3(left, (high_ref[start:stop, :stop], low_ref[start:stop, :stop]), transposed=True)
            for block in range(start // LANES, stop // LANES):
                at = LANES * block - start
                out_ref[pl.ds(block, ORDER, stride=BLOCKS), :] = result[:, at:at + LANES]

    @pl.when(jnp.logical_and(row >= col, col > 0))
    def _():
        load(row_ref, row_high, row_low)
        load(col_ref, col_high, col_low)
        for start, stop in reversed(GROUPS):
            weights = high_ref[start:stop, :stop], low_ref[start:stop, :stop]
            solved = product3(weights, (row_high[:stop, :], row_low[:stop, :]))
            left_high[:, start:stop], left_low[:, start:stop] = split(solved.T)
            solved = product3(weights, (col_high[:stop, :], col_low[:stop, :]))
            col_high[start:stop, :], col_low[start:stop, :] = split(solved)
        added = jnp.where(row == col, damping_ref[0], 0.0)
        row_id = lax.broadcasted_iota(jnp.int32, (ORDER, LANES), 0)
        lane_id = lax.broadcasted_iota(jnp.int32, (ORDER, LANES), 1)
        for start, stop in GROUPS:
            left = left_high[...], left_low[...]
            result = product3(left, (col_high[:, start:stop], col_low[:, start:stop]))
            for block in range(start // LANES, stop // LANES):
                at = LANES * block - start
                place = pl.ds(block, ORDER, stride=BLOCKS)
                own = own_ref[place, :]
                own = jnp.where(row_id == lane_id + LANES * block, own + added, own)
                out_ref[place, :] = own - result[:, at:at + LANES]


VMEM = pl.BlockSpec(memory_space=pltpu.VMEM)
SMEM = pl.BlockSpec(memory_space=pltpu.SMEM)


def factorize(where, damping, pairs):
    return pl.pallas_call(
        factor_kernel,
        out_shape=[
            jax.ShapeDtypeStruct((ORDER, ORDER), BF16),
            jax.ShapeDtypeStruct((ORDER, ORDER), BF16),
            jax.ShapeDtypeStruct((ORDER, ORDER), F32),
        ],
        in_specs=[SMEM, SMEM] + [VMEM] * CHIPS,
        out_specs=[VMEM, VMEM, VMEM],
        scratch_shapes=[pltpu.VMEM((ORDER, ORDER), F32)],
        interpret=INTERPRET,
        name="factorize",
    )(where, damping, *pairs)


def finish(where, damping, high, low, upper, row_tile, col_tile, own):
    return pl.pallas_call(
        update_kernel,
        out_shape=jax.ShapeDtypeStruct((FLAT, LANES), F32),
        in_specs=[SMEM, SMEM] + [VMEM] * 6,
        out_specs=VMEM,
        scratch_shapes=[pltpu.VMEM((ORDER, ORDER), BF16)] * 6,
        interpret=INTERPRET,
        name="finish",
    )(where, damping, high, low, upper, row_tile, col_tile, own)


def spread(own):
    row = lax.axis_index("row")
    col = lax.axis_index("col")
    core = row % 2
    chips = GRID // 2
    size = own.shape[0] // chips

    piece = jnp.where(row == 0, own[:size], 0.0)
    arrived = [
        lax.ppermute(own[size * z:size * (z + 1)], "row", [(0, 2 * z)]) for z in SCATTER
    ]
    for other in arrived:
        piece = piece + other

    second = lax.ppermute(piece[size // 2:], "row", [(2 * z, 2 * z + 1) for z in range(chips)])
    half = jnp.where(core == 0, piece[:size // 2], second)
    col_tile = lax.all_gather(half, "row", axis=0, tiled=True)
    swap = [(r * GRID + c, c * GRID + r) for r in range(GRID) for c in range(GRID)]
    turned = lax.ppermute(half, ("row", "col"), swap)

    moving = jnp.where(col == 0, piece, 0.0)
    for hop in (8, 4, 2, 1):
        moving = moving + lax.ppermute(
            moving, ("row", "col"),
            [(2 * z * GRID + c, 2 * z * GRID + c + hop) for z in range(chips) for c in range(0, GRID, 2 * hop)],
        )
    moving = moving + lax.ppermute(moving, "row", [(2 * z, 2 * z + 1) for z in range(chips)])

    other_core = [(r, r ^ 1) for r in range(GRID)]
    onward = [(2 * z, 2 * ((z + 1) % chips)) for z in range(chips)]
    onward += [(2 * z + 1, 2 * ((z - 1) % chips) + 1) for z in range(chips)]
    pairs = [moving]
    for hop in range(1, chips // 2 + 1):
        moving = lax.ppermute(moving, "row", onward)
        if hop == 3:
            moving, turned = lax.optimization_barrier((moving, turned))
        pairs.append(moving)
        if hop < chips // 2:
            pairs.append(lax.ppermute(moving, "row", other_core))
    row_tile = lax.all_gather(turned, "col", axis=0, tiled=True)
    return pairs, row_tile, col_tile


def on_device(factor, damping):
    row = lax.axis_index("row")
    col = lax.axis_index("col")
    own = factor.reshape(FLAT, LANES)
    pairs, row_tile, col_tile = spread(own)
    where = jnp.stack([row, col]).astype(jnp.int32)
    high, low, upper = factorize(where, damping, pairs)
    result = finish(where, damping, high, low, upper, row_tile, col_tile, own)
    return result.reshape(factor.shape)


def solution(mesh):
    return jax.shard_map(
        on_device,
        mesh=mesh,
        in_specs=(P(None, "row", None, None, "col", None), P()),
        out_specs=P(None, "row", None, None, "col", None),
        check_vma=False,
    )
```

```python
import jax
import jax.numpy as jnp
from jax import lax
from jax.experimental import pallas as pl
from jax.experimental.pallas import tpu as pltpu
from jax.sharding import PartitionSpec as P


F32 = jnp.float32
BF16 = jnp.bfloat16
ORDER = 896
LANES = 128
BLOCKS = ORDER // LANES
FLAT = ORDER * BLOCKS
GRID = 16
CHIPS = GRID // 2
PIECE_ROWS = ORDER // GRID
GROUPS = ((0, 256), (256, 512), (512, 768), (768, 896))
SCATTER = (4, 3, 5, 2, 6, 1, 7)
INTERPRET = False


def split(value):
    high = value.astype(BF16)
    return high, (value - high.astype(F32)).astype(BF16)


def product(left, right, transposed):
    dims = (((1,), (1 if transposed else 0,)), ((), ()))
    return lax.dot_general(left, right, dims, preferred_element_type=F32)


def product3(left, right, transposed=False):
    (left_high, left_low), (right_high, right_low) = left, right
    return product(left_high, right_high, transposed) + (
        product(left_high, right_low, transposed) + product(left_low, right_high, transposed)
    )


def factor_block(rows):
    lane = lax.broadcasted_iota(jnp.int32, (8, LANES), 1)
    sublane = lax.broadcasted_iota(jnp.int32, (8, LANES), 0)

    def lane_of(value, index):
        return jnp.broadcast_to(value[:, index:index + 1], (8, LANES))

    def row_of(value, index):
        return jnp.broadcast_to(value[index:index + 1, :], (8, LANES))

    rows = list(rows)
    mixed, corner = [], []
    for slab in range(16):
        base = 8 * slab
        own = (lane >= base) & (lane < base + 8)
        pivot_rows = rows[slab]
        columns = [lane_of(pivot_rows, base + m) for m in range(8)]
        diag_rows = jnp.where(own, pivot_rows, 0.0)
        pivot_rows = jnp.where(own, jnp.where(lane - base == sublane, 1.0, 0.0), pivot_rows)
        mixed_slab = jnp.zeros((8, LANES), F32)
        corner_slab = jnp.zeros((8, LANES), F32)
        for j in range(8):
            pivot = row_of(columns[j], j)
            root = lax.rsqrt(pivot)
            inverse = 1.0 / pivot
            is_j = sublane == j
            factor = jnp.where(is_j, 1.0 - inverse, columns[j] * inverse)
            mixed_slab = jnp.where(is_j, pivot_rows * root, mixed_slab)
            corner_slab = jnp.where(is_j, diag_rows * root, corner_slab)
            for m in range(j + 1, 8):
                columns[m] = columns[m] - factor * row_of(columns[m], j)
            pivot_rows = pivot_rows - factor * row_of(pivot_rows, j)
            if j < 7:
                diag_rows = diag_rows - factor * row_of(diag_rows, j)
        mixed.append(mixed_slab)
        corner.append(corner_slab)
        spread = [row_of(pivot_rows, m) for m in range(8)]
        for other in range(slab + 1, min(slab + 3, 16)):
            old = rows[other]
            new = jnp.where(own, 0.0, old)
            for m in range(8):
                new = new - lane_of(old, base + m) * spread[m]
            rows[other] = new
        far = range(slab + 3, 16)
        if far:
            blank = jnp.zeros((8, LANES), F32)
            placed = jnp.concatenate([pivot_rows if i == slab else blank for i in range(16)], axis=0)
            lanes = jnp.concatenate([jnp.where(own, rows[i], 0.0) for i in far], axis=0)
            change = product3(split(lanes), split(placed))
            for at, i in enumerate(far):
                rows[i] = jnp.where(own, 0.0, rows[i]) - change[8 * at:8 * at + 8]
    return mixed, corner


def factor_kernel(where_ref, damping_ref, *refs):
    piece_refs, (high_ref, low_ref, upper_ref, work) = refs[:GRID], refs[GRID:]
    damping = damping_ref[0]
    chip = where_ref[0] // 2
    core = where_ref[0] % 2
    row_id = lax.broadcasted_iota(jnp.int32, (PIECE_ROWS, LANES), 0)
    lane_id = lax.broadcasted_iota(jnp.int32, (PIECE_ROWS, LANES), 1)
    for index, ref in enumerate(piece_refs):
        distance, other = piece_of(index)
        source = 2 * ((chip + distance + CHIPS) % CHIPS) + (1 - core if other else core)
        start = pl.multiple_of(source * PIECE_ROWS, PIECE_ROWS)
        for block in range(BLOCKS):
            values = ref[pl.ds(block, PIECE_ROWS, stride=BLOCKS), :]
            on_diagonal = row_id + start == lane_id + LANES * block
            work[pl.ds(start, PIECE_ROWS), LANES * block:LANES * (block + 1)] = jnp.where(
                on_diagonal, values + damping, values
            )
    lane = lax.broadcasted_iota(jnp.int32, (8, LANES), 1)

    def step(k, carry):
        start = pl.multiple_of(k * LANES, LANES)
        here = pl.ds(start, LANES)
        slabs = [work[pl.ds(start + 8 * i, 8), here] for i in range(16)]
        mixed, corner = factor_block(slabs)
        inverse = jnp.concatenate([jnp.where(lane < 8 * i + 8, mixed[i], 0.0) for i in range(16)], axis=0)
        upper = jnp.concatenate([jnp.where(lane < 8 * i + 8, corner[i], mixed[i]) for i in range(16)], axis=0)
        inverse_parts = split(inverse)
        work[here, :] = product3(inverse_parts, split(work[here, :]))
        upper_ref[here, :] = work[here, :]
        upper_ref[here, here] = upper
        work[here, here] = inverse
        panel_parts = split(work[here, :])

        def update(i, inner):
            there = pl.ds(pl.multiple_of(i * LANES, LANES), LANES)
            column = product3(split(work[there, here]), inverse_parts, transposed=True)
            work[there, here] = jnp.zeros((LANES, LANES), F32)
            work[there, :] = work[there, :] - product3(split(column), panel_parts)
            return inner

        lax.fori_loop(k + 1, BLOCKS, update, 0)
        return carry

    lax.fori_loop(0, BLOCKS, step, 0)
    for i in range(BLOCKS):
        down = slice(LANES * i, LANES * (i + 1))
        row_id = lax.broadcasted_iota(jnp.int32, (LANES, ORDER), 0) + LANES * i
        col_id = lax.broadcasted_iota(jnp.int32, (LANES, ORDER), 1)
        high, low = split(jnp.where(col_id <= row_id, work[down, :], 0.0))
        high_ref[down, :] = high
        low_ref[down, :] = low


def update_kernel(
    where_ref, damping_ref, high_ref, low_ref, upper_ref, row_ref, col_ref, own_ref, out_ref,
    row_high, row_low, col_high, col_low, left_high, left_low,
):
    row, col = where_ref[0], where_ref[1]

    def load(ref, high, low):
        for block in range(BLOCKS):
            lanes = slice(LANES * block, LANES * (block + 1))
            high[:, lanes], low[:, lanes] = split(ref[pl.ds(block, ORDER, stride=BLOCKS), :])

    @pl.when(row < col)
    def _():
        out_ref[...] = jnp.zeros((FLAT, LANES), F32)

    @pl.when(jnp.logical_and(row == 0, col == 0))
    def _():
        row_id = lax.broadcasted_iota(jnp.int32, (ORDER, LANES), 0)
        lane_id = lax.broadcasted_iota(jnp.int32, (ORDER, LANES), 1)
        for block in range(BLOCKS):
            lower = upper_ref[LANES * block:LANES * (block + 1), :].T
            keep = row_id >= lane_id + LANES * block
            out_ref[pl.ds(block, ORDER, stride=BLOCKS), :] = jnp.where(keep, lower, 0.0)

    @pl.when(jnp.logical_and(row >= col, row > 0))
    def _():
        load(row_ref, row_high, row_low)
        for start, stop in GROUPS:
            weights = high_ref[start:stop, :stop], low_ref[start:stop, :stop]
            solved = product3(weights, (row_high[:stop, :], row_low[:stop, :])).T
            left_high[:, start:stop], left_low[:, start:stop] = split(solved)

            @pl.when(col == 0)
            def _():
                for block in range(start // LANES, stop // LANES):
                    at = LANES * block - start
                    out_ref[pl.ds(block, ORDER, stride=BLOCKS), :] = solved[:, at:at + LANES]

    @pl.when(jnp.logical_and(row >= col, col > 0))
    def _():
        load(col_ref, col_high, col_low)
        for start, stop in reversed(GROUPS):
            weights = high_ref[start:stop, :stop], low_ref[start:stop, :stop]
            solved = product3(weights, (col_high[:stop, :], col_low[:stop, :]))
            col_high[start:stop, :], col_low[start:stop, :] = split(solved)
        added = jnp.where(row == col, damping_ref[0], 0.0)
        row_id = lax.broadcasted_iota(jnp.int32, (ORDER, LANES), 0)
        lane_id = lax.broadcasted_iota(jnp.int32, (ORDER, LANES), 1)
        for start, stop in GROUPS:
            left = left_high[...], left_low[...]
            result = product3(left, (col_high[:, start:stop], col_low[:, start:stop]))
            for block in range(start // LANES, stop // LANES):
                at = LANES * block - start
                place = pl.ds(block, ORDER, stride=BLOCKS)
                own = own_ref[place, :]
                own = jnp.where(row_id == lane_id + LANES * block, own + added, own)
                out_ref[place, :] = own - result[:, at:at + LANES]


VMEM = pl.BlockSpec(memory_space=pltpu.VMEM)
SMEM = pl.BlockSpec(memory_space=pltpu.SMEM)


def factorize(where, damping, pieces):
    return pl.pallas_call(
        factor_kernel,
        out_shape=[
            jax.ShapeDtypeStruct((ORDER, ORDER), BF16),
            jax.ShapeDtypeStruct((ORDER, ORDER), BF16),
            jax.ShapeDtypeStruct((ORDER, ORDER), F32),
        ],
        in_specs=[SMEM, SMEM] + [VMEM] * GRID,
        out_specs=[VMEM, VMEM, VMEM],
        scratch_shapes=[pltpu.VMEM((ORDER, ORDER), F32)],
        interpret=INTERPRET,
        name="factorize",
    )(where, damping, *pieces)


def finish(where, damping, high, low, upper, row_tile, col_tile, own):
    return pl.pallas_call(
        update_kernel,
        out_shape=jax.ShapeDtypeStruct((FLAT, LANES), F32),
        in_specs=[SMEM, SMEM] + [VMEM] * 6,
        out_specs=VMEM,
        scratch_shapes=[pltpu.VMEM((ORDER, ORDER), BF16)] * 6,
        interpret=INTERPRET,
        name="finish",
    )(where, damping, high, low, upper, row_tile, col_tile, own)


def spread(own):
    row = lax.axis_index("row")
    col = lax.axis_index("col")
    core = row % 2
    chips = GRID // 2
    size = own.shape[0] // chips

    piece = jnp.where(row == 0, own[:size], 0.0)
    arrived = []
    source = own
    for z in SCATTER:
        part, source = lax.optimization_barrier((source[size * z:size * (z + 1)], source))
        arrived.append(lax.ppermute(part, "row", [(0, 2 * z)]))
    for other in arrived:
        piece = piece + other

    second = lax.ppermute(piece[size // 2:], "row", [(2 * z, 2 * z + 1) for z in range(chips)])
    half = jnp.where(core == 0, piece[:size // 2], second)
    col_tile = lax.all_gather(half, "row", axis=0, tiled=True)
    swap = [(r * GRID + c, c * GRID + r) for r in range(GRID) for c in range(GRID)]
    turned = lax.ppermute(half, ("row", "col"), swap)

    moving = jnp.where(col == 0, half, 0.0)
    for hop in (8, 4, 2, 1):
        moving = moving + lax.ppermute(moving, "col", [(c, c + hop) for c in range(0, GRID, 2 * hop)])

    def step(value, pairs):
        return lax.ppermute(value, "row", pairs)

    forth = [(r, (r + 2) % GRID) for r in range(GRID)]
    back = [(r, (r - 2) % GRID) for r in range(GRID)]
    across = [(r, r ^ 1) for r in range(GRID)]
    ahead = behind = moving
    pieces = [moving, step(moving, across)]
    for hop in range(1, chips // 2):
        ahead = step(ahead, forth)
        behind = step(behind, back)
        if hop == 3:
            behind, turned = lax.optimization_barrier((behind, turned))
        pieces += [ahead, step(ahead, across), behind, step(behind, across)]
    ahead = step(ahead, forth)
    pieces += [ahead, step(ahead, across)]
    row_tile = lax.all_gather(turned, "col", axis=0, tiled=True)
    return pieces, row_tile, col_tile


def piece_of(index):
    if index < 2:
        return 0, index
    hop, kind = (index - 2) // 4 + 1, (index - 2) % 4
    return (-hop, hop)[kind // 2], kind % 2


def on_device(factor, damping):
    row = lax.axis_index("row")
    col = lax.axis_index("col")
    own = factor.reshape(FLAT, LANES)
    pieces, row_tile, col_tile = spread(own)
    where = jnp.stack([row, col]).astype(jnp.int32)
    high, low, upper = factorize(where, damping, pieces)
    result = finish(where, damping, high, low, upper, row_tile, col_tile, own)
    return result.reshape(factor.shape)


def solution(mesh):
    return jax.shard_map(
        on_device,
        mesh=mesh,
        in_specs=(P(None, "row", None, None, "col", None), P()),
        out_specs=P(None, "row", None, None, "col", None),
        check_vma=False,
    )
```

```python
import jax
import jax.numpy as jnp
from jax import lax
from jax.experimental import pallas as pl
from jax.experimental.pallas import tpu as pltpu
from jax.sharding import PartitionSpec as P


F32 = jnp.float32
BF16 = jnp.bfloat16
ORDER = 896
LANES = 128
BLOCKS = ORDER // LANES
FLAT = ORDER * BLOCKS
GRID = 16
CHIPS = GRID // 2
PIECE_ROWS = ORDER // GRID
GROUPS = ((0, 256), (256, 512), (512, 768), (768, 896))
SCATTER = (4, 3, 5, 2, 6, 1, 7)
INTERPRET = False


def split(value):
    high = value.astype(BF16)
    return high, (value - high.astype(F32)).astype(BF16)


def product(left, right, transposed):
    dims = (((1,), (1 if transposed else 0,)), ((), ()))
    return lax.dot_general(left, right, dims, preferred_element_type=F32)


def product3(left, right, transposed=False):
    (left_high, left_low), (right_high, right_low) = left, right
    return product(left_high, right_high, transposed) + (
        product(left_high, right_low, transposed) + product(left_low, right_high, transposed)
    )


def factor_block(rows):
    lane = lax.broadcasted_iota(jnp.int32, (8, LANES), 1)
    sublane = lax.broadcasted_iota(jnp.int32, (8, LANES), 0)

    def lane_of(value, index):
        return jnp.broadcast_to(value[:, index:index + 1], (8, LANES))

    def row_of(value, index):
        return jnp.broadcast_to(value[index:index + 1, :], (8, LANES))

    rows = list(rows)
    mixed, corner = [], []
    for slab in range(16):
        base = 8 * slab
        own = (lane >= base) & (lane < base + 8)
        pivot_rows = rows[slab]
        columns = [lane_of(pivot_rows, base + m) for m in range(8)]
        diag_rows = jnp.where(own, pivot_rows, 0.0)
        pivot_rows = jnp.where(own, jnp.where(lane - base == sublane, 1.0, 0.0), pivot_rows)
        mixed_slab = jnp.zeros((8, LANES), F32)
        corner_slab = jnp.zeros((8, LANES), F32)
        for j in range(8):
            pivot = row_of(columns[j], j)
            root = lax.rsqrt(pivot)
            inverse = 1.0 / pivot
            is_j = sublane == j
            factor = jnp.where(is_j, 1.0 - inverse, columns[j] * inverse)
            mixed_slab = jnp.where(is_j, pivot_rows * root, mixed_slab)
            corner_slab = jnp.where(is_j, diag_rows * root, corner_slab)
            for m in range(j + 1, 8):
                columns[m] = columns[m] - factor * row_of(columns[m], j)
            pivot_rows = pivot_rows - factor * row_of(pivot_rows, j)
            if j < 7:
                diag_rows = diag_rows - factor * row_of(diag_rows, j)
        mixed.append(mixed_slab)
        corner.append(corner_slab)
        spread = [row_of(pivot_rows, m) for m in range(8)]
        for other in range(slab + 1, min(slab + 3, 16)):
            old = rows[other]
            new = jnp.where(own, 0.0, old)
            for m in range(8):
                new = new - lane_of(old, base + m) * spread[m]
            rows[other] = new
        far = range(slab + 3, 16)
        if far:
            blank = jnp.zeros((8, LANES), F32)
            placed = jnp.concatenate([pivot_rows if i == slab else blank for i in range(16)], axis=0)
            lanes = jnp.concatenate([jnp.where(own, rows[i], 0.0) for i in far], axis=0)
            change = product3(split(lanes), split(placed))
            for at, i in enumerate(far):
                rows[i] = jnp.where(own, 0.0, rows[i]) - change[8 * at:8 * at + 8]
    return mixed, corner


def load_turned(ref, high, low):
    for block in range(BLOCKS):
        down = slice(LANES * block, LANES * (block + 1))
        high[down, :], low[down, :] = split(ref[pl.ds(block, ORDER, stride=BLOCKS), :].T)


def solve(tile, inverse, start, stop):
    (high, low), (inverse_high, inverse_low) = tile, inverse
    weights = inverse_high[start:stop, :stop], inverse_low[start:stop, :stop]
    return product3((high[:, :stop], low[:, :stop]), weights, transposed=True)


def factor_kernel(where_ref, damping_ref, *refs):
    piece_refs, col_ref, (high_ref, low_ref, upper_ref, right_high, right_low) = refs[:GRID], refs[GRID], refs[GRID + 1:GRID + 6]
    work, left_high, left_low, panel, tile_high, tile_low = refs[GRID + 6:]
    damping = damping_ref[0]
    chip = where_ref[0] // 2
    core = where_ref[0] % 2
    row_id = lax.broadcasted_iota(jnp.int32, (PIECE_ROWS, LANES), 0)
    lane_id = lax.broadcasted_iota(jnp.int32, (PIECE_ROWS, LANES), 1)
    for index, ref in enumerate(piece_refs):
        distance, other = piece_of(index)
        source = 2 * ((chip + distance + CHIPS) % CHIPS) + (1 - core if other else core)
        start = pl.multiple_of(source * PIECE_ROWS, PIECE_ROWS)
        for block in range(BLOCKS):
            values = ref[pl.ds(block, PIECE_ROWS, stride=BLOCKS), :]
            on_diagonal = row_id + start == lane_id + LANES * block
            work[pl.ds(start, PIECE_ROWS), LANES * block:LANES * (block + 1)] = jnp.where(
                on_diagonal, values + damping, values
            )
    lane = lax.broadcasted_iota(jnp.int32, (8, LANES), 1)

    def step(k, carry):
        start = pl.multiple_of(k * LANES, LANES)
        here = pl.ds(start, LANES)
        slabs = [work[pl.ds(start + 8 * i, 8), here] for i in range(16)]
        mixed, corner = factor_block(slabs)
        inverse = jnp.concatenate([jnp.where(lane < 8 * i + 8, mixed[i], 0.0) for i in range(16)], axis=0)
        upper = jnp.concatenate([jnp.where(lane < 8 * i + 8, corner[i], mixed[i]) for i in range(16)], axis=0)
        high, low = split(inverse)
        stacked = jnp.concatenate([high, low], axis=1)
        column_high, column_low = split(work[:, here])
        column = product(jnp.concatenate([column_high, column_high], axis=1), stacked, True)
        column = column + product(column_low, high, True)
        left_high[...], left_low[...] = split(column)
        work[here, :] = product3((high, low), split(work[here, :]))
        upper_ref[here, :] = work[here, :]
        upper_ref[here, here] = upper
        work[here, here] = inverse
        high, low = split(work[here, :])
        panel[:LANES, :] = high
        panel[LANES:, :] = low

        def update(i, inner):
            there = pl.ds(pl.multiple_of(i * LANES, LANES), LANES)
            left = left_high[there, :]
            change = product(jnp.concatenate([left, left], axis=1), panel[...], False)
            change = change + product(left_low[there, :], panel[:LANES, :], False)
            work[there, here] = jnp.zeros((LANES, LANES), F32)
            work[there, :] = work[there, :] - change
            return inner

        lax.fori_loop(k + 1, BLOCKS, update, 0)
        return carry

    lax.fori_loop(0, BLOCKS, step, 0)
    for i in range(BLOCKS):
        down = slice(LANES * i, LANES * (i + 1))
        row_id = lax.broadcasted_iota(jnp.int32, (LANES, ORDER), 0) + LANES * i
        col_id = lax.broadcasted_iota(jnp.int32, (LANES, ORDER), 1)
        high, low = split(jnp.where(col_id <= row_id, work[down, :], 0.0))
        high_ref[down, :] = high
        low_ref[down, :] = low

    @pl.when(jnp.logical_and(where_ref[0] >= where_ref[1], where_ref[1] > 0))
    def _():
        load_turned(col_ref, tile_high, tile_low)
        for start, stop in GROUPS:
            solved = solve((tile_high, tile_low), (high_ref, low_ref), start, stop).T
            right_high[start:stop, :], right_low[start:stop, :] = split(solved)


def update_kernel(
    where_ref, damping_ref, high_ref, low_ref, upper_ref, right_high, right_low, row_ref, own_ref, out_ref,
    tile_high, tile_low, left_high, left_low,
):
    row, col = where_ref[0], where_ref[1]

    @pl.when(row < col)
    def _():
        out_ref[...] = jnp.zeros((FLAT, LANES), F32)

    @pl.when(jnp.logical_and(row == 0, col == 0))
    def _():
        row_id = lax.broadcasted_iota(jnp.int32, (ORDER, LANES), 0)
        lane_id = lax.broadcasted_iota(jnp.int32, (ORDER, LANES), 1)
        for block in range(BLOCKS):
            lower = upper_ref[LANES * block:LANES * (block + 1), :].T
            keep = row_id >= lane_id + LANES * block
            out_ref[pl.ds(block, ORDER, stride=BLOCKS), :] = jnp.where(keep, lower, 0.0)

    @pl.when(jnp.logical_and(row >= col, row > 0))
    def _():
        load_turned(row_ref, tile_high, tile_low)
        for start, stop in GROUPS:
            solved = solve((tile_high, tile_low), (high_ref, low_ref), start, stop)
            left_high[:, start:stop], left_low[:, start:stop] = split(solved)

            for block in range(start // LANES, stop // LANES):
                at = LANES * block - start
                out_ref[pl.ds(block, ORDER, stride=BLOCKS), :] = solved[:, at:at + LANES]

    @pl.when(jnp.logical_and(row >= col, col > 0))
    def _():
        added = jnp.where(row == col, damping_ref[0], 0.0)
        row_id = lax.broadcasted_iota(jnp.int32, (ORDER, LANES), 0)
        lane_id = lax.broadcasted_iota(jnp.int32, (ORDER, LANES), 1)
        for start, stop in GROUPS:
            left = left_high[...], left_low[...]
            result = product3(left, (right_high[:, start:stop], right_low[:, start:stop]))
            for block in range(start // LANES, stop // LANES):
                at = LANES * block - start
                place = pl.ds(block, ORDER, stride=BLOCKS)
                own = own_ref[place, :]
                own = jnp.where(row_id == lane_id + LANES * block, own + added, own)
                out_ref[place, :] = own - result[:, at:at + LANES]


VMEM = pl.BlockSpec(memory_space=pltpu.VMEM)
SMEM = pl.BlockSpec(memory_space=pltpu.SMEM)


def factorize(where, damping, pieces, col_tile):
    return pl.pallas_call(
        factor_kernel,
        out_shape=[
            jax.ShapeDtypeStruct((ORDER, ORDER), BF16),
            jax.ShapeDtypeStruct((ORDER, ORDER), BF16),
            jax.ShapeDtypeStruct((ORDER, ORDER), F32),
            jax.ShapeDtypeStruct((ORDER, ORDER), BF16),
            jax.ShapeDtypeStruct((ORDER, ORDER), BF16),
        ],
        in_specs=[SMEM, SMEM] + [VMEM] * (GRID + 1),
        out_specs=[VMEM] * 5,
        scratch_shapes=[
            pltpu.VMEM((ORDER, ORDER), F32),
            pltpu.VMEM((ORDER, LANES), BF16),
            pltpu.VMEM((ORDER, LANES), BF16),
            pltpu.VMEM((2 * LANES, ORDER), BF16),
            pltpu.VMEM((ORDER, ORDER), BF16),
            pltpu.VMEM((ORDER, ORDER), BF16),
        ],
        interpret=INTERPRET,
        name="factorize",
    )(where, damping, *pieces, col_tile)


def finish(where, damping, factors, row_tile, own):
    return pl.pallas_call(
        update_kernel,
        out_shape=jax.ShapeDtypeStruct((FLAT, LANES), F32),
        in_specs=[SMEM, SMEM] + [VMEM] * 7,
        out_specs=VMEM,
        scratch_shapes=[pltpu.VMEM((ORDER, ORDER), BF16)] * 4,
        interpret=INTERPRET,
        name="finish",
    )(where, damping, *factors, row_tile, own)


def spread(own):
    row = lax.axis_index("row")
    col = lax.axis_index("col")
    core = row % 2
    chips = GRID // 2
    size = own.shape[0] // chips

    piece = jnp.where(row == 0, own[:size], 0.0)
    arrived = []
    source = own
    for z in SCATTER:
        part, source = lax.optimization_barrier((source[size * z:size * (z + 1)], source))
        arrived.append(lax.ppermute(part, "row", [(0, 2 * z)]))
    for other in arrived:
        piece = piece + other

    second = lax.ppermute(piece[size // 2:], "row", [(2 * z, 2 * z + 1) for z in range(chips)])
    half = jnp.where(core == 0, piece[:size // 2], second)
    col_tile = lax.all_gather(half, "row", axis=0, tiled=True)
    swap = [(r * GRID + c, c * GRID + r) for r in range(GRID) for c in range(GRID)]
    turned = lax.ppermute(half, ("row", "col"), swap)

    moving = jnp.where(col == 0, half, 0.0)
    for hop in (8, 4, 2, 1):
        moving = moving + lax.ppermute(moving, "col", [(c, c + hop) for c in range(0, GRID, 2 * hop)])

    def step(value, pairs):
        return lax.ppermute(value, "row", pairs)

    forth = [(r, (r + 2) % GRID) for r in range(GRID)]
    back = [(r, (r - 2) % GRID) for r in range(GRID)]
    across = [(r, r ^ 1) for r in range(GRID)]
    ahead = behind = moving
    pieces = [moving, step(moving, across)]
    for hop in range(1, chips // 2):
        ahead = step(ahead, forth)
        behind = step(behind, back)
        if hop == 3:
            behind, turned = lax.optimization_barrier((behind, turned))
        pieces += [ahead, step(ahead, across), behind, step(behind, across)]
    ahead = step(ahead, forth)
    pieces += [ahead, step(ahead, across)]
    row_tile = lax.all_gather(turned, "col", axis=0, tiled=True)
    return pieces, row_tile, col_tile


def piece_of(index):
    if index < 2:
        return 0, index
    hop, kind = (index - 2) // 4 + 1, (index - 2) % 4
    return (-hop, hop)[kind // 2], kind % 2


def on_device(factor, damping):
    row = lax.axis_index("row")
    col = lax.axis_index("col")
    own = factor.reshape(FLAT, LANES)
    pieces, row_tile, col_tile = spread(own)
    where = jnp.stack([row, col]).astype(jnp.int32)
    factors = factorize(where, damping, pieces, col_tile)
    result = finish(where, damping, factors, row_tile, own)
    return result.reshape(factor.shape)


def solution(mesh):
    return jax.shard_map(
        on_device,
        mesh=mesh,
        in_specs=(P(None, "row", None, None, "col", None), P()),
        out_specs=P(None, "row", None, None, "col", None),
        check_vma=False,
    )
```

```python
import jax
import jax.numpy as jnp
from jax import lax
from jax.experimental import pallas as pl
from jax.experimental.pallas import tpu as pltpu
from jax.sharding import PartitionSpec as P


F32 = jnp.float32
BF16 = jnp.bfloat16
ORDER = 896
LANES = 128
BLOCKS = ORDER // LANES
FLAT = ORDER * BLOCKS
GRID = 16
CHIPS = GRID // 2
PIECE_ROWS = ORDER // GRID
GROUPS = ((0, 256), (256, 512), (512, 768), (768, 896))
SCATTER = (4, 3, 5, 2, 6, 1, 7)
INTERPRET = False


def split(value):
    high = value.astype(BF16)
    return high, (value - high.astype(F32)).astype(BF16)


def product(left, right, transposed):
    dims = (((1,), (1 if transposed else 0,)), ((), ()))
    return lax.dot_general(left, right, dims, preferred_element_type=F32)


def product3(left, right, transposed=False):
    (left_high, left_low), (right_high, right_low) = left, right
    return product(left_high, right_high, transposed) + (
        product(left_high, right_low, transposed) + product(left_low, right_high, transposed)
    )


def factor_block(rows):
    lane = lax.broadcasted_iota(jnp.int32, (8, LANES), 1)
    sublane = lax.broadcasted_iota(jnp.int32, (8, LANES), 0)

    def lane_of(value, index):
        return jnp.broadcast_to(value[:, index:index + 1], (8, LANES))

    def row_of(value, index):
        return jnp.broadcast_to(value[index:index + 1, :], (8, LANES))

    rows = list(rows)
    mixed, corner = [], []
    for slab in range(16):
        base = 8 * slab
        own = (lane >= base) & (lane < base + 8)
        pivot_rows = rows[slab]
        columns = [lane_of(pivot_rows, base + m) for m in range(8)]
        diag_rows = jnp.where(own, pivot_rows, 0.0)
        pivot_rows = jnp.where(own, jnp.where(lane - base == sublane, 1.0, 0.0), pivot_rows)
        mixed_slab = jnp.zeros((8, LANES), F32)
        corner_slab = jnp.zeros((8, LANES), F32)
        for j in range(8):
            pivot = row_of(columns[j], j)
            root = lax.rsqrt(pivot)
            inverse = 1.0 / pivot
            is_j = sublane == j
            factor = jnp.where(is_j, 1.0 - inverse, columns[j] * inverse)
            mixed_slab = jnp.where(is_j, pivot_rows * root, mixed_slab)
            corner_slab = jnp.where(is_j, diag_rows * root, corner_slab)
            for m in range(j + 1, 8):
                columns[m] = columns[m] - factor * row_of(columns[m], j)
            pivot_rows = pivot_rows - factor * row_of(pivot_rows, j)
            if j < 7:
                diag_rows = diag_rows - factor * row_of(diag_rows, j)
        mixed.append(mixed_slab)
        corner.append(corner_slab)
        spread = [row_of(pivot_rows, m) for m in range(8)]
        for other in range(slab + 1, min(slab + 3, 16)):
            old = rows[other]
            new = jnp.where(own, 0.0, old)
            for m in range(8):
                new = new - lane_of(old, base + m) * spread[m]
            rows[other] = new
        far = range(slab + 3, 16)
        if far:
            blank = jnp.zeros((8, LANES), F32)
            placed = jnp.concatenate([pivot_rows if i == slab else blank for i in range(16)], axis=0)
            lanes = jnp.concatenate([jnp.where(own, rows[i], 0.0) for i in far], axis=0)
            change = product3(split(lanes), split(placed))
            for at, i in enumerate(far):
                rows[i] = jnp.where(own, 0.0, rows[i]) - change[8 * at:8 * at + 8]
    return mixed, corner


def load_turned(ref, high, low):
    for block in range(BLOCKS):
        down = slice(LANES * block, LANES * (block + 1))
        high[down, :], low[down, :] = split(ref[pl.ds(block, ORDER, stride=BLOCKS), :].T)


def solve(tile, inverse, start, stop):
    (high, low), (inverse_high, inverse_low) = tile, inverse
    weights = inverse_high[start:stop, :stop], inverse_low[start:stop, :stop]
    return product3((high[:, :stop], low[:, :stop]), weights, transposed=True)


def factor_kernel(where_ref, damping_ref, *refs):
    piece_refs, col_ref, (high_ref, low_ref, upper_ref, right_high, right_low) = refs[:GRID], refs[GRID], refs[GRID + 1:GRID + 6]
    work, left_high, left_low, panel, tile_high, tile_low = refs[GRID + 6:]
    damping = damping_ref[0]
    chip = where_ref[0] // 2
    core = where_ref[0] % 2
    row_id = lax.broadcasted_iota(jnp.int32, (PIECE_ROWS, LANES), 0)
    lane_id = lax.broadcasted_iota(jnp.int32, (PIECE_ROWS, LANES), 1)
    for index, ref in enumerate(piece_refs):
        distance, other = piece_of(index)
        source = 2 * ((chip + distance + CHIPS) % CHIPS) + (1 - core if other else core)
        start = pl.multiple_of(source * PIECE_ROWS, PIECE_ROWS)
        for block in range(BLOCKS):
            values = ref[pl.ds(block, PIECE_ROWS, stride=BLOCKS), :]
            on_diagonal = row_id + start == lane_id + LANES * block
            work[pl.ds(start, PIECE_ROWS), LANES * block:LANES * (block + 1)] = jnp.where(
                on_diagonal, values + damping, values
            )
    lane = lax.broadcasted_iota(jnp.int32, (8, LANES), 1)

    def step(k, carry):
        start = pl.multiple_of(k * LANES, LANES)
        here = pl.ds(start, LANES)
        slabs = [work[pl.ds(start + 8 * i, 8), here] for i in range(16)]
        mixed, corner = factor_block(slabs)
        inverse = jnp.concatenate([jnp.where(lane < 8 * i + 8, mixed[i], 0.0) for i in range(16)], axis=0)
        upper = jnp.concatenate([jnp.where(lane < 8 * i + 8, corner[i], mixed[i]) for i in range(16)], axis=0)
        high, low = split(inverse)
        stacked = jnp.concatenate([high, low], axis=1)
        column_high, column_low = split(work[:, here])
        column = product(jnp.concatenate([column_high, column_high], axis=1), stacked, True)
        column = column + product(column_low, high, True)
        left_high[...], left_low[...] = split(column)
        work[here, :] = product3((high, low), split(work[here, :]))
        upper_ref[here, :] = work[here, :]
        upper_ref[here, here] = upper
        work[here, here] = inverse
        high, low = split(work[here, :])
        panel[:LANES, :] = high
        panel[LANES:, :] = low

        def update(i, inner):
            there = pl.ds(pl.multiple_of(i * LANES, LANES), LANES)
            left = left_high[there, :]
            change = product(jnp.concatenate([left, left], axis=1), panel[...], False)
            change = change + product(left_low[there, :], panel[:LANES, :], False)
            work[there, here] = jnp.zeros((LANES, LANES), F32)
            work[there, :] = work[there, :] - change
            return inner

        lax.fori_loop(k + 1, BLOCKS, update, 0)
        return carry

    lax.fori_loop(0, BLOCKS, step, 0)
    for i in range(BLOCKS):
        down = slice(LANES * i, LANES * (i + 1))
        row_id = lax.broadcasted_iota(jnp.int32, (LANES, ORDER), 0) + LANES * i
        col_id = lax.broadcasted_iota(jnp.int32, (LANES, ORDER), 1)
        high, low = split(jnp.where(col_id <= row_id, work[down, :], 0.0))
        high_ref[down, :] = high
        low_ref[down, :] = low

    @pl.when(jnp.logical_and(where_ref[0] >= where_ref[1], where_ref[1] > 0))
    def _():
        load_turned(col_ref, tile_high, tile_low)
        for start, stop in GROUPS:
            solved = solve((tile_high, tile_low), (high_ref, low_ref), start, stop).T
            right_high[start:stop, :], right_low[start:stop, :] = split(solved)


def update_kernel(
    where_ref, damping_ref, high_ref, low_ref, upper_ref, right_high, right_low, row_ref, own_ref, out_ref,
    tile_high, tile_low, left_high, left_low,
):
    row, col = where_ref[0], where_ref[1]

    @pl.when(row < col)
    def _():
        out_ref[...] = jnp.zeros((FLAT, LANES), F32)

    @pl.when(jnp.logical_and(row == 0, col == 0))
    def _():
        row_id = lax.broadcasted_iota(jnp.int32, (ORDER, LANES), 0)
        lane_id = lax.broadcasted_iota(jnp.int32, (ORDER, LANES), 1)
        for block in range(BLOCKS):
            lower = upper_ref[LANES * block:LANES * (block + 1), :].T
            keep = row_id >= lane_id + LANES * block
            out_ref[pl.ds(block, ORDER, stride=BLOCKS), :] = jnp.where(keep, lower, 0.0)

    @pl.when(jnp.logical_and(row >= col, row > 0))
    def _():
        load_turned(row_ref, tile_high, tile_low)
        for start, stop in GROUPS:
            solved = solve((tile_high, tile_low), (high_ref, low_ref), start, stop)
            left_high[:, start:stop], left_low[:, start:stop] = split(solved)

            for block in range(start // LANES, stop // LANES):
                at = LANES * block - start
                out_ref[pl.ds(block, ORDER, stride=BLOCKS), :] = solved[:, at:at + LANES]

    @pl.when(jnp.logical_and(row >= col, col > 0))
    def _():
        added = jnp.where(row == col, damping_ref[0], 0.0)
        row_id = lax.broadcasted_iota(jnp.int32, (ORDER, LANES), 0)
        lane_id = lax.broadcasted_iota(jnp.int32, (ORDER, LANES), 1)
        for start, stop in GROUPS:
            left = left_high[...], left_low[...]
            result = product3(left, (right_high[:, start:stop], right_low[:, start:stop]))
            for block in range(start // LANES, stop // LANES):
                at = LANES * block - start
                place = pl.ds(block, ORDER, stride=BLOCKS)
                own = own_ref[place, :]
                own = jnp.where(row_id == lane_id + LANES * block, own + added, own)
                out_ref[place, :] = own - result[:, at:at + LANES]


VMEM = pl.BlockSpec(memory_space=pltpu.VMEM)
SMEM = pl.BlockSpec(memory_space=pltpu.SMEM)


def factorize(where, damping, pieces, col_tile):
    return pl.pallas_call(
        factor_kernel,
        out_shape=[
            jax.ShapeDtypeStruct((ORDER, ORDER), BF16),
            jax.ShapeDtypeStruct((ORDER, ORDER), BF16),
            jax.ShapeDtypeStruct((ORDER, ORDER), F32),
            jax.ShapeDtypeStruct((ORDER, ORDER), BF16),
            jax.ShapeDtypeStruct((ORDER, ORDER), BF16),
        ],
        in_specs=[SMEM, SMEM] + [VMEM] * (GRID + 1),
        out_specs=[VMEM] * 5,
        scratch_shapes=[
            pltpu.VMEM((ORDER, ORDER), F32),
            pltpu.VMEM((ORDER, LANES), BF16),
            pltpu.VMEM((ORDER, LANES), BF16),
            pltpu.VMEM((2 * LANES, ORDER), BF16),
            pltpu.VMEM((ORDER, ORDER), BF16),
            pltpu.VMEM((ORDER, ORDER), BF16),
        ],
        interpret=INTERPRET,
        name="factorize",
    )(where, damping, *pieces, col_tile)


def finish(where, damping, factors, row_tile, own):
    return pl.pallas_call(
        update_kernel,
        out_shape=jax.ShapeDtypeStruct((FLAT, LANES), F32),
        in_specs=[SMEM, SMEM] + [VMEM] * 7,
        out_specs=VMEM,
        scratch_shapes=[pltpu.VMEM((ORDER, ORDER), BF16)] * 4,
        interpret=INTERPRET,
        name="finish",
    )(where, damping, *factors, row_tile, own)


def spread(own):
    row = lax.axis_index("row")
    col = lax.axis_index("col")
    core = row % 2
    chips = GRID // 2
    size = own.shape[0] // chips

    arrived = []
    source = own
    for z in SCATTER:
        part, source = lax.optimization_barrier((source[size * z:size * (z + 1)], source))
        arrived.append(lax.ppermute(part, "row", [(0, 2 * z)]))
    source, arrived[0] = lax.optimization_barrier((own, arrived[0]))
    piece = jnp.where(row == 0, source[:size], 0.0)
    for other in arrived:
        piece = piece + other

    second = lax.ppermute(piece[size // 2:], "row", [(2 * z, 2 * z + 1) for z in range(chips)])
    half = jnp.where(core == 0, piece[:size // 2], second)
    col_tile = lax.all_gather(half, "row", axis=0, tiled=True)
    swap = [(r * GRID + c, c * GRID + r) for r in range(GRID) for c in range(GRID)]
    turned = lax.ppermute(half, ("row", "col"), swap)

    moving = jnp.where(col == 0, half, 0.0)
    for hop in (8, 4, 2, 1):
        moving = moving + lax.ppermute(moving, "col", [(c, c + hop) for c in range(0, GRID, 2 * hop)])

    def step(value, pairs):
        return lax.ppermute(value, "row", pairs)

    forth = [(r, (r + 2) % GRID) for r in range(GRID)]
    back = [(r, (r - 2) % GRID) for r in range(GRID)]
    across = [(r, r ^ 1) for r in range(GRID)]
    ahead = behind = moving
    pieces = [moving, step(moving, across)]
    for hop in range(1, chips // 2):
        ahead = step(ahead, forth)
        behind = step(behind, back)
        if hop == 2:
            behind, turned = lax.optimization_barrier((behind, turned))
        pieces += [ahead, step(ahead, across), behind, step(behind, across)]
    ahead = step(ahead, forth)
    pieces += [ahead, step(ahead, across)]
    row_tile = lax.all_gather(turned, "col", axis=0, tiled=True)
    return pieces, row_tile, col_tile


def piece_of(index):
    if index < 2:
        return 0, index
    hop, kind = (index - 2) // 4 + 1, (index - 2) % 4
    return (-hop, hop)[kind // 2], kind % 2


def on_device(factor, damping):
    row = lax.axis_index("row")
    col = lax.axis_index("col")
    own = factor.reshape(FLAT, LANES)
    pieces, row_tile, col_tile = spread(own)
    where = jnp.stack([row, col]).astype(jnp.int32)
    factors = factorize(where, damping, pieces, col_tile)
    result = finish(where, damping, factors, row_tile, own)
    return result.reshape(factor.shape)


def solution(mesh):
    return jax.shard_map(
        on_device,
        mesh=mesh,
        in_specs=(P(None, "row", None, None, "col", None), P()),
        out_specs=P(None, "row", None, None, "col", None),
        check_vma=False,
    )
```
